256 devices in a mesh: node: 32 (over z_hi, y, x), query: 8 (over z_lo, core).
Axes of the slice: x: 4, y: 4, z: 8 (z_hi: 2, z_lo: 4; z = z_hi * 4 + z_lo), core: 2. Of those that a mesh axis runs over, the one named last changes fastest.
Arguments:
- state: float32 [32768, 2048], P('node', 'query'), may hold values from -6 to 6
- tiles: bfloat16 [12288, 128, 128], P(('node', 'query')), may hold values from -0.119628906 to 0.119628906
- tile_src: int32 [12288], P(('node', 'query')), may hold values from 0 to 7
- tile_dst: int32 [12288], P(('node', 'query')), may hold values from 0 to 256, as said below
- tile_rel: int32 [12288], P(('node', 'query')), may hold values from 0 to 1314
- query_src: int32 [32], P('query'), may hold values from 0 to 32767
- query_rel: int32 [32], P('query'), may hold values from 0 to 1314
- rel_table: float32 [1315, 64], replicated, may hold values from -6 to 6
- query_table: float32 [1315, 64], replicated, may hold values from -6 to 6
- linear_weight: float32 [64, 64], replicated, may hold values from -0.75 to 0.75
- linear_bias: float32 [64], replicated, may hold values from -3 to 3
- norm_gain: float32 [64], replicated, may hold values from 0.25 to 1.75
- norm_shift: float32 [64], replicated, may hold values from -3 to 3
Outputs:
- updated: float32 [32768, 2048], P('node', 'query')
The draws below stay inside these ranges and needn't reach their ends.
Inputs may be any that keep to these rules, and one draw needn't show every extreme that they name: `tile_dst`: in each node shard's list of 384 slots (its devices' slots in query order) the used slots come first. The number of used slots of a shard is 384 divided by 1, 2, 4 or 8 (rounded down); some shard uses all its slots and some other uses an eighth.
All inputs are finite; a program needn't handle non-finite values.
Results may differ from the reference program's by a relative error of at most 0.01.
Values may be sent and summed in bfloat16 or wider, within the bound.
No kernel may reach another device: no remote copies, remote signals or barrier semaphores. Data moves between devices by JAX's collectives and lax.ppermute only.
A program may use at most 192 MiB of HBM per device.

```python
import jax
import jax.numpy as jnp
from jax import lax

C = 64
R = 1315
TILE = 128
TCAP = 48
NODES = 32768
QUERIES = 32
NBLK = 256
SRC_BLK = 8
SHARD_SLOTS = 384
SLOTS = 12288
N_NODE = 32
N_QUERY = 8


def draw_tile_dst(key, part):
    key_level, key_full, key_target = jax.random.split(jax.random.fold_in(key, 7), 3)
    shards = SLOTS // SHARD_SLOTS
    levels = jax.random.randint(key_level, (shards,), 0, 4)
    counts = jnp.right_shift(jnp.full((shards,), SHARD_SLOTS, jnp.int32), levels.astype(jnp.int32))
    full_shard = jax.random.randint(key_full, (), 0, shards)
    counts = counts.at[(full_shard + 1) % shards].set(SHARD_SLOTS // 8)
    counts = counts.at[full_shard].set(SHARD_SLOTS)
    targets = jax.random.randint(key_target, (SLOTS,), 0, NBLK)
    slot_ids = jnp.arange(SLOTS, dtype=jnp.int32)
    used = slot_ids % SHARD_SLOTS < counts[slot_ids // SHARD_SLOTS]
    return jnp.where(used, targets, NBLK).astype(jnp.int32)


def plant(result, rng, least, high):
    dims = result.shape
    index_at = [jax.random.randint(jax.random.fold_in(rng, axis), (), 0, dims[axis]) for axis in range(len(dims))]
    result = result.at[tuple(index_at)].set(least)
    longest = dims.index(max(dims))
    index_at[longest] = (index_at[longest] + 1) % dims[longest]
    return result.at[tuple(index_at)].set(high)


def block_levels(own_key, extent, cuts, least, top_value):
    factor_of, own = 1.0, jax.random.fold_in(own_key, 6)
    for position, blocks in cuts:
        heights = jnp.exp(jax.random.uniform(jax.random.fold_in(own, position), (blocks,), jnp.float32, least / len(cuts), top_value / len(cuts)))
        factor_of = factor_of * jnp.repeat(heights, extent[position] // blocks).reshape([-1 if axis == position else 1 for axis in range(len(extent))])
    return factor_of


def bell_draw(own_key, extent, scale, most, cuts=(), kind=jnp.bfloat16):
    gain = block_levels(own_key, extent, cuts, -0.22, 0.18) if cuts else 1.0
    entries = jax.random.normal(own_key, extent, jnp.float32) * scale * gain
    return jnp.minimum(jnp.maximum(entries, -most), most).astype(kind)


def setup_inputs(seed: int = 0) -> dict:
    keys = jax.random.split(jax.random.key(seed), 14)
    state = bell_draw(keys[0], (NODES, QUERIES * C), 1.0, 6.0, ((0, 32), (1, 8)), jnp.float32)
    tiles = bell_draw(keys[1], (SLOTS, TILE, TILE), 0.02, 0.119628906, ((0, 256),))
    tile_src = plant(jax.random.randint(keys[2], (SLOTS,), 0, SRC_BLK), jax.random.fold_in(keys[2], 1), 0, SRC_BLK - 1).astype(jnp.int32)
    tile_dst = draw_tile_dst(jax.random.fold_in(keys[13], 71), 0)
    tile_rel = plant(jax.random.randint(keys[4], (SLOTS,), 0, R), jax.random.fold_in(keys[4], 1), 0, R - 1).astype(jnp.int32)
    query_src = plant(jax.random.randint(keys[5], (QUERIES,), 0, NODES), jax.random.fold_in(keys[5], 1), 0, NODES - 1).astype(jnp.int32)
    query_rel = plant(jax.random.randint(keys[6], (QUERIES,), 0, R), jax.random.fold_in(keys[6], 1), 0, R - 1).astype(jnp.int32)
    rel_table = bell_draw(keys[7], (R, C), 1.0, 6.0, (), jnp.float32)
    query_table = bell_draw(keys[8], (R, C), 1.0, 6.0, (), jnp.float32)
    linear_weight = bell_draw(keys[9], (C, C), C ** -0.5, 0.75, (), jnp.float32)
    linear_bias = bell_draw(keys[10], (C,), 0.5, 3.0, (), jnp.float32)
    norm_gain = jnp.clip(1.0 + 0.15 * jax.random.normal(keys[11], (C,), jnp.float32), 0.25, 1.75)
    norm_shift = bell_draw(keys[12], (C,), 0.5, 3.0, (), jnp.float32)
    return {"state": state, "tiles": tiles, "tile_src": tile_src, "tile_dst": tile_dst, "tile_rel": tile_rel, "query_src": query_src, "query_rel": query_rel, "rel_table": rel_table, "query_table": query_table, "linear_weight": linear_weight, "linear_bias": linear_bias, "norm_gain": norm_gain, "norm_shift": norm_shift}


def reference(state, tiles, tile_src, tile_dst, tile_rel, query_src, query_rel, rel_table, query_table, linear_weight, linear_bias, norm_gain, norm_shift):
    width = QUERIES * C
    state_bf = state.astype(jnp.bfloat16)
    source_blocks = state_bf.reshape(NBLK, TILE, width)
    query_vectors = query_table[query_rel]
    shard_tiles = tiles.reshape(N_NODE, N_QUERY, TCAP, TILE, TILE)
    shard_src = tile_src.reshape(N_NODE, N_QUERY, TCAP)
    shard_dst = tile_dst.reshape(N_NODE, N_QUERY, TCAP)
    shard_rel = tile_rel.reshape(N_NODE, N_QUERY, TCAP)

    def shard_step(message, inputs):
        shard, block_tiles, block_src, block_dst, block_rel = inputs

        def block_step(partial_value, block):
            pieces, sources, targets, relations = block
            usable = targets < NBLK

            def add_terms(current):
                source_rows = source_blocks[shard * SRC_BLK + sources]
                product = jnp.einsum('btu,buc->btc', pieces.astype(jnp.float32), source_rows.astype(jnp.float32))
                scales = (rel_table[relations][:, None, :] * query_vectors[None, :, :]).reshape(TCAP, width)
                term = product * scales[:, None, :] * usable.astype(jnp.float32)[:, None, None]
                return current.at[jnp.minimum(targets, NBLK - 1)].add(term)
            return (lax.cond(jnp.any(usable), add_terms, lambda current: current, partial_value), None)
        partial_value, _ = lax.scan(block_step, jnp.zeros((NBLK, TILE, width), jnp.float32), (block_tiles, block_src, block_dst, block_rel))
        rounded = lax.optimization_barrier(partial_value.astype(jnp.bfloat16)).astype(jnp.float32)
        return (message + rounded, None)
    shards = jnp.arange(N_NODE, dtype=jnp.int32)
    message, _ = lax.scan(shard_step, jnp.zeros((NBLK, TILE, width), jnp.float32), (shards, shard_tiles, shard_src, shard_dst, shard_rel))
    message = message.reshape(NODES, QUERIES, C)
    node_ids = jnp.arange(NODES, dtype=jnp.int32)
    hits = (node_ids[:, None] == query_src[None, :]).astype(jnp.float32)
    aggregate = message + hits[:, :, None] * query_vectors[None, :, :]
    mapped = jnp.einsum('nqc,cd->nqd', aggregate, linear_weight, precision=lax.Precision.HIGHEST) + linear_bias
    center = lax.optimization_barrier(jnp.mean(mapped, axis=-1, keepdims=True))
    spread = lax.optimization_barrier(jnp.mean((mapped - center) ** 2, axis=-1, keepdims=True))
    normed = norm_gain * (mapped - center) / jnp.sqrt(spread + 1e-05) + norm_shift
    return jnp.maximum(normed, 0.0).reshape(NODES, width)
```

```python
import jax
import jax.numpy as jnp
from jax import lax
from jax.experimental import pallas as pl
from jax.experimental.pallas import tpu as pltpu
from jax.sharding import Mesh
from jax.sharding import PartitionSpec as P

GROUP = 8
DEPTH = 6
PARTS = 2
CHUNK = 16


def message_kernel(order, srcs, pos, seg, tiles, state, scales, out, buf, acc, sems, *, first_chunk):
    tile = tiles.shape[1]
    chunk = first_chunk + pl.program_id(0)
    begin = seg[first_chunk]
    start = seg[chunk]
    stop = seg[chunk + 1]
    last_all = seg[first_chunk + pl.num_programs(0)]
    groups = (stop - start + GROUP - 1) // GROUP

    def slots_of(group):
        return [jnp.minimum(start + group * GROUP + i, stop - 1) for i in range(GROUP)]

    def fetch(group):
        ring = lax.rem(group, DEPTH)
        for i, k in enumerate(slots_of(group)):
            pltpu.make_async_copy(tiles.at[order[k]], buf.at[ring * GROUP + i], sems.at[ring]).start()

    out[...] = jnp.zeros_like(out)
    del begin, last_all

    @pl.when(pl.program_id(0) == 0)
    def _():
        acc[...] = jnp.zeros_like(acc)

    def prime(group, carry):
        fetch(group)
        return carry

    lax.fori_loop(0, jnp.minimum(groups, DEPTH - 1), prime, 0)

    def step(group, carry):
        @pl.when(group + DEPTH - 1 < groups)
        def _():
            fetch(group + DEPTH - 1)

        ring = lax.rem(group, DEPTH)
        pltpu.make_async_copy(
            tiles.at[pl.ds(0, GROUP)], buf.at[pl.ds(ring * GROUP, GROUP)], sems.at[ring]
        ).wait()
        total = acc[...]
        for i, k in enumerate(slots_of(group)):
            valid = start + group * GROUP + i < stop
            here = pos[k]
            before = pos[jnp.maximum(k - 1, 0)]
            fresh = jnp.logical_and(valid, jnp.logical_or(k == start, here != before))
            keep = jnp.where(fresh, 0.0, 1.0).astype(jnp.float32)
            live = jnp.where(valid, 1.0, 0.0).astype(jnp.float32)
            source = pl.multiple_of(srcs[k] * tile, tile)
            product = jnp.dot(
                buf[ring * GROUP + i],
                state[pl.ds(source, tile), :],
                preferred_element_type=jnp.float32,
            )
            total = product * (scales[pl.ds(k, 1), :] * live) + total * keep
            row = pl.multiple_of((here - chunk * CHUNK) * tile, tile)
            out[pl.ds(row, tile), :] = total.astype(out.dtype)
        acc[...] = total
        return carry

    lax.fori_loop(0, groups, step, 0)


def messages(order, srcs, pos, seg, tiles, state, scales, part):
    slots, tile, _ = tiles.shape
    width = state.shape[1]
    chunks = (seg.shape[0] - 1) // PARTS
    return pl.pallas_call(
        lambda *refs: message_kernel(*refs, first_chunk=part * chunks),
        grid_spec=pltpu.PrefetchScalarGridSpec(
            num_scalar_prefetch=4,
            grid=(chunks,),
            in_specs=[
                pl.BlockSpec(memory_space=pl.ANY),
                pl.BlockSpec(state.shape, lambda i, *_: (0, 0)),
                pl.BlockSpec(scales.shape, lambda i, *_: (0, 0)),
            ],
            out_specs=pl.BlockSpec((CHUNK * tile, width), lambda i, *_: (i, 0)),
            scratch_shapes=[
                pltpu.VMEM((DEPTH * GROUP, tile, tile), jnp.bfloat16),
                pltpu.VMEM((tile, width), jnp.float32),
                pltpu.SemaphoreType.DMA((DEPTH,)),
            ],
        ),
        out_shape=jax.ShapeDtypeStruct((chunks * CHUNK * tile, width), jnp.bfloat16),
        name=f"messages_{part}",
    )(order, srcs, pos, seg, tiles, state, scales)


def update_kernel(
    base, own0, own1, got0, got1, query_src, query_row, weight, average, rows, out
):
    count = own0.shape[0]
    width = own0.shape[1]
    channels = width // query_src.shape[0]
    for part, (own, got) in enumerate(((own0, got0), (own1, got1))):
        first = base[0] + part * count
        node = lax.broadcasted_iota(jnp.int32, (count, width), 0) + first
        query = lax.broadcasted_iota(jnp.int32, (1, width), 1) // channels
        target = jnp.zeros((1, width), jnp.int32)
        for q in range(query_src.shape[0]):
            target = jnp.where(query == q, query_src[q], target)
        aggregate = own[...].astype(jnp.float32) + got[...].astype(jnp.float32)
        aggregate = aggregate + jnp.where(node == target, query_row[...], 0.0)
        mapped = (
            jnp.dot(aggregate, weight[...], precision=lax.Precision.HIGHEST, preferred_element_type=jnp.float32)
            + rows[0:1, :]
        )
        center = jnp.dot(mapped, average[...], precision=lax.Precision.HIGHEST, preferred_element_type=jnp.float32)
        shifted = mapped - center
        spread = jnp.dot(
            shifted * shifted, average[...], precision=lax.Precision.HIGHEST, preferred_element_type=jnp.float32
        )
        normed = rows[1:2, :] * shifted / jnp.sqrt(spread + 1e-05) + rows[2:3, :]
        out[pl.ds(part * count, count), :] = jnp.maximum(normed, 0.0)


def update(base, owns, gots, query_src, query_row, weight, average, rows):
    count, width = owns[0].shape
    smem = pl.BlockSpec(memory_space=pltpu.SMEM)
    vmem = pl.BlockSpec(memory_space=pltpu.VMEM)
    return pl.pallas_call(
        update_kernel,
        in_specs=[smem, vmem, vmem, vmem, vmem, smem, vmem, vmem, vmem, vmem],
        out_specs=vmem,
        out_shape=jax.ShapeDtypeStruct((count * PARTS, width), jnp.float32),
        name="update",
    )(base, *owns, *gots, query_src, query_row, weight, average, rows)


def local(
    state,
    tiles,
    tile_src,
    tile_dst,
    tile_rel,
    query_src,
    query_rel,
    rel_table,
    query_table,
    linear_weight,
    linear_bias,
    norm_gain,
    norm_shift,
):
    node_rows, width = state.shape
    tile = tiles.shape[1]
    channels = rel_table.shape[1]
    queries = width // channels
    owned = node_rows // tile
    outer = lax.axis_size("zh")
    inner = lax.axis_size("y") * lax.axis_size("x")
    owners = outer * inner
    blocks = owned * owners

    lists = lax.all_gather(jnp.stack([tile_src, tile_dst, tile_rel]), ("zl", "c"), axis=1, tiled=True)
    src, dst, rel = lists[0], lists[1], lists[2]
    slot_tiles = lax.all_gather(tiles, ("zl", "c"), axis=0, tiled=True)

    each = owned // PARTS
    owner = dst // owned
    inside = dst % owned
    place = ((inside // each * inner + owner % inner) * outer + owner // inner) * each + inside % each
    place = jnp.where(dst < blocks, place, blocks)
    slots = src.shape[0]
    ids = jnp.arange(slots, dtype=jnp.int32)
    key = place * slots + ids
    rank = jnp.sum((key[None, :] < key[:, None]).astype(jnp.int32), axis=1)
    chosen = rank[None, :] == ids[:, None]

    def sorted_by_place(values):
        return jnp.sum(jnp.where(chosen, values[None, :], 0), axis=1)

    order = sorted_by_place(ids)
    srcs = sorted_by_place(src)
    pos = sorted_by_place(place)
    rels = sorted_by_place(rel)
    edges = jnp.arange(blocks // CHUNK + 1, dtype=jnp.int32) * CHUNK
    seg = jnp.sum((place[None, :] < edges[:, None]).astype(jnp.int32), axis=1)

    query_row = query_table[query_rel].reshape(1, width)
    scales = jnp.tile(rel_table[rels], (1, queries)) * query_row
    state_bf = state.astype(jnp.bfloat16)

    node = lax.axis_index("zh")
    owns, gots = [], []
    for part in range(PARTS):
        partial = messages(order, srcs, pos, seg, slot_tiles, state_bf, scales, part)
        summed = lax.psum_scatter(partial, ("y", "x"), scatter_dimension=0, tiled=True)
        summed = summed.reshape(outer, each * tile, width)
        owns.append(lax.dynamic_index_in_dim(summed, node, 0, keepdims=False))
        away = lax.dynamic_index_in_dim(summed, outer - 1 - node, 0, keepdims=False)
        gots.append(lax.ppermute(away, "zh", [(0, 1), (1, 0)]))

    eye = jnp.eye(queries, dtype=jnp.float32)
    weight = jnp.kron(eye, linear_weight)
    average = jnp.kron(eye, jnp.full((channels, channels), 1.0 / channels, jnp.float32))
    rows = jnp.stack(
        [jnp.tile(linear_bias, queries), jnp.tile(norm_gain, queries), jnp.tile(norm_shift, queries)]
    )
    shard = (lax.axis_index("zh") * lax.axis_size("y") + lax.axis_index("y")) * lax.axis_size("x") + lax.axis_index("x")
    base = (shard * node_rows).astype(jnp.int32).reshape(1)
    return update(base, owns, gots, query_src, query_row, weight, average, rows)


def solution(mesh):
    fine = Mesh(mesh.devices.reshape(2, 4, 4, 4, 2), ("zh", "y", "x", "zl", "c"))
    node = ("zh", "y", "x")
    query = ("zl", "c")
    placed = (
        P(node, query),
        P(node + query, None, None),
        P(node + query),
        P(node + query),
        P(node + query),
        P(query),
        P(query),
        P(),
        P(),
        P(),
        P(),
        P(),
        P(),
    )
    return jax.shard_map(local, mesh=fine, in_specs=placed, out_specs=P(node, query), check_vma=False)
```

```python
import jax
import jax.numpy as jnp
from jax import lax
from jax.experimental import pallas as pl
from jax.experimental.pallas import tpu as pltpu
from jax.sharding import Mesh
from jax.sharding import PartitionSpec as P

GROUP = 8
DEPTH = 8
UNIT = 16


def message_kernel(order, srcs, locs, fresh, seg, tiles, state, scales, *rest, first, count):
    outs = rest[:-5]
    each = count // len(outs)
    buf, acc, obuf, sems, osems = rest[-5:]
    tile = tiles.shape[1]
    rows = obuf.shape[1] - tile
    step_id = pl.program_id(0)
    begin = seg[first]
    end = seg[first + count]
    start = seg[first + step_id]
    stop = seg[first + step_id + 1]

    def fetch(group):
        ring = lax.rem(group, DEPTH)
        for i in range(GROUP):
            pltpu.make_async_copy(
                tiles.at[order[group * GROUP + i]], buf.at[ring * GROUP + i], sems.at[ring]
            ).start()

    @pl.when(step_id == 0)
    def _():
        acc[...] = jnp.zeros_like(acc)

        def prime(group, carry):
            fetch(group)
            return carry

        lax.fori_loop(begin, jnp.minimum(end, begin + DEPTH - 1), prime, 0)

    side = lax.rem(step_id, 2)

    def put(n, s):
        return pltpu.make_async_copy(
            obuf.at[s, pl.ds(0, rows)], outs[n // each].at[pl.ds(n % each * rows, rows)], osems.at[s]
        )

    for n in range(2, count):

        @pl.when(step_id == n)
        def _(n=n):
            put(n - 2, n % 2).wait()

    obuf[side] = jnp.zeros(obuf.shape[1:], obuf.dtype)

    def step(group, carry):
        @pl.when(group + DEPTH - 1 < end)
        def _():
            fetch(group + DEPTH - 1)

        ring = lax.rem(group, DEPTH)
        pltpu.make_async_copy(
            tiles.at[pl.ds(0, GROUP)], buf.at[pl.ds(ring * GROUP, GROUP)], sems.at[ring]
        ).wait()
        total = acc[...]
        for i in range(GROUP):
            k = group * GROUP + i
            keep = jnp.where(fresh[k] > 0, 0.0, 1.0).astype(jnp.float32)
            source = pl.multiple_of(srcs[k] * tile, tile)
            product = jnp.dot(
                buf[ring * GROUP + i],
                state[pl.ds(source, tile), :],
                preferred_element_type=jnp.float32,
            )
            total = product * scales[pl.ds(k, 1), :] + total * keep
            row = pl.multiple_of(locs[k] * tile, tile)
            obuf[side, pl.ds(row, tile), :] = total.astype(obuf.dtype)
        acc[...] = total
        return carry

    lax.fori_loop(start, stop, step, 0)

    for n in range(count):

        @pl.when(step_id == n)
        def _(n=n):
            put(n, n % 2).start()

    @pl.when(step_id == count - 1)
    def _():
        for n in range(max(count - 2, 0), count):
            put(n, n % 2).wait()


def messages(lists, tiles, state, scales, first, count, outs):
    order, srcs, locs, fresh, seg = lists
    _, tile, _ = tiles.shape
    width = state.shape[1]
    rows = UNIT * tile
    return pl.pallas_call(
        lambda *refs: message_kernel(*refs, first=first, count=count),
        grid_spec=pltpu.PrefetchScalarGridSpec(
            num_scalar_prefetch=5,
            grid=(count,),
            in_specs=[
                pl.BlockSpec(memory_space=pl.ANY),
                pl.BlockSpec(state.shape, lambda i, *_: (0, 0)),
                pl.BlockSpec(scales.shape, lambda i, *_: (0, 0)),
            ],
            out_specs=[pl.BlockSpec(memory_space=pl.ANY)] * outs,
            scratch_shapes=[
                pltpu.VMEM((DEPTH * GROUP, tile, tile), jnp.bfloat16),
                pltpu.VMEM((tile, width), jnp.float32),
                pltpu.VMEM((2, rows + tile, width), jnp.bfloat16),
                pltpu.SemaphoreType.DMA((DEPTH,)),
                pltpu.SemaphoreType.DMA((2,)),
            ],
        ),
        out_shape=[jax.ShapeDtypeStruct((count // outs * rows, width), jnp.bfloat16)] * outs,
        name=f"messages_{first}",
    )(order, srcs, locs, fresh, seg, tiles, state, scales)


def update_kernel(base, owns, gots, query_src, query_row, weight, average, rows, out):
    width = owns[0].shape[1]
    channels = width // query_src.shape[0]
    query = lax.broadcasted_iota(jnp.int32, (1, width), 1) // channels
    target = jnp.zeros((1, width), jnp.int32)
    for q in range(query_src.shape[0]):
        target = jnp.where(query == q, query_src[q], target)
    done = 0
    for own, got in zip(owns, gots):
        count = own.shape[0]
        first = base[0] + done
        node = lax.broadcasted_iota(jnp.int32, (count, width), 0) + first
        aggregate = own[...].astype(jnp.float32) + got[...].astype(jnp.float32)
        aggregate = aggregate + jnp.where(node == target, query_row[...], 0.0)
        mapped = (
            jnp.dot(aggregate, weight[...], precision=lax.Precision.HIGHEST, preferred_element_type=jnp.float32)
            + rows[0:1, :]
        )
        center = jnp.dot(mapped, average[...], precision=lax.Precision.HIGHEST, preferred_element_type=jnp.float32)
        shifted = mapped - center
        spread = jnp.dot(
            shifted * shifted, average[...], precision=lax.Precision.HIGHEST, preferred_element_type=jnp.float32
        )
        normed = rows[1:2, :] * shifted / jnp.sqrt(spread + 1e-05) + rows[2:3, :]
        out[pl.ds(done, count), :] = jnp.maximum(normed, 0.0)
        done += count


def update(base, owns, gots, query_src, query_row, weight, average, rows):
    parts = len(owns)
    width = owns[0].shape[1]
    total = sum(own.shape[0] for own in owns)
    smem = pl.BlockSpec(memory_space=pltpu.SMEM)
    vmem = pl.BlockSpec(memory_space=pltpu.VMEM)

    def kernel(base, *refs):
        update_kernel(base, refs[:parts], refs[parts : 2 * parts], *refs[2 * parts :])

    return pl.pallas_call(
        kernel,
        in_specs=[smem] + [vmem] * (2 * parts) + [smem, vmem, vmem, vmem, vmem],
        out_specs=vmem,
        out_shape=jax.ShapeDtypeStruct((total, width), jnp.float32),
        name="update",
    )(base, *owns, *gots, query_src, query_row, weight, average, rows)


def shift(value, axis, by):
    size = lax.axis_size(axis)
    return lax.ppermute(value, axis, [(i, (i + by) % size) for i in range(size)])


def local(
    state,
    tiles,
    tile_src,
    tile_dst,
    tile_rel,
    query_src,
    query_rel,
    rel_table,
    query_table,
    linear_weight,
    linear_bias,
    norm_gain,
    norm_shift,
):
    node_rows, width = state.shape
    tile = tiles.shape[1]
    channels = rel_table.shape[1]
    queries = width // channels
    owned = node_rows // tile
    outer, ny, nx = lax.axis_size("zh"), lax.axis_size("y"), lax.axis_size("x")
    owners = outer * ny * nx
    blocks = owned * owners
    at_z, at_y, at_x = lax.axis_index("zh"), lax.axis_index("y"), lax.axis_index("x")

    lists = lax.all_gather(jnp.stack([tile_src, tile_dst, tile_rel]), ("zl", "c"), axis=1, tiled=True)
    src, dst, rel = lists[0], lists[1], lists[2]
    slot_tiles = lax.all_gather(tiles, ("zl", "c"), axis=0, tiled=True)

    owner, inside = dst // owned, dst % owned
    go_z = (owner // (ny * nx) - at_z) % outer
    used = dst < blocks
    bins = blocks // UNIT
    place = jnp.where(used, (owner % (ny * nx) * outer + go_z) * owned + inside, blocks)
    bin_id = place // UNIT
    loc = place % UNIT
    unit = UNIT

    slots = src.shape[0]
    ids = jnp.arange(slots, dtype=jnp.int32)
    key = place * slots + ids
    below = key[None, :] < key[:, None]
    rank = jnp.sum(below.astype(jnp.int32), axis=1)
    same = jnp.logical_and(below, place[None, :] == place[:, None])
    first_here = jnp.logical_not(jnp.any(same, axis=1)).astype(jnp.int32)
    edges = jnp.arange(bins + 1, dtype=jnp.int32)
    ahead = jnp.sum((place[None, :] < (edges * unit)[:, None]).astype(jnp.int32), axis=1)
    groups = (ahead[1:] - ahead[:-1] + GROUP - 1) // GROUP
    seg = jnp.sum(jnp.where(edges[None, :-1] < edges[:, None], groups[None, :], 0), axis=1)
    moved = seg[:-1] * GROUP - ahead[:-1]
    move = jnp.sum(jnp.where(jnp.minimum(bin_id, bins - 1)[:, None] == edges[None, :-1], moved[None, :], 0), axis=1)
    padded = slots + bins * GROUP
    goal = jnp.where(used, rank + move, padded)
    chosen = goal[None, :] == jnp.arange(padded, dtype=jnp.int32)[:, None]

    def placed_at(values, fill):
        return jnp.sum(jnp.where(chosen, (values - fill)[None, :], 0), axis=1) + fill

    order = placed_at(ids, 0)
    srcs = placed_at(src, 0)
    locs = placed_at(loc, unit)
    fresh = placed_at(first_here, 0)
    rels = placed_at(rel, 0)
    filled = jnp.any(chosen, axis=1)
    work = (order, srcs, locs, fresh, seg)

    query_row = query_table[query_rel].reshape(1, width)
    scales = jnp.tile(jnp.where(filled[:, None], rel_table[rels], 0.0), (1, queries)) * query_row
    state_bf = state.astype(jnp.bfloat16)

    (partial,) = messages(work, slot_tiles, state_bf, scales, 0, bins, 1)
    summed = lax.psum_scatter(partial, ("y", "x"), scatter_dimension=0, tiled=True)
    owns = [summed[:node_rows]]
    gots = [shift(summed[node_rows:], "zh", 1)]

    eye = jnp.eye(queries, dtype=jnp.float32)
    weight = jnp.kron(eye, linear_weight)
    average = jnp.kron(eye, jnp.full((channels, channels), 1.0 / channels, jnp.float32))
    rows = jnp.stack(
        [jnp.tile(linear_bias, queries), jnp.tile(norm_gain, queries), jnp.tile(norm_shift, queries)]
    )
    shard = (at_z * ny + at_y) * nx + at_x
    first_node = (shard * node_rows).astype(jnp.int32).reshape(1)
    return update(first_node, owns, gots, query_src, query_row, weight, average, rows)


def solution(mesh):
    fine = Mesh(mesh.devices.reshape(2, 4, 4, 4, 2), ("zh", "y", "x", "zl", "c"))
    node = ("zh", "y", "x")
    query = ("zl", "c")
    placed = (
        P(node, query),
        P(node + query, None, None),
        P(node + query),
        P(node + query),
        P(node + query),
        P(query),
        P(query),
        P(),
        P(),
        P(),
        P(),
        P(),
        P(),
    )
    return jax.shard_map(local, mesh=fine, in_specs=placed, out_specs=P(node, query), check_vma=False)
```

```python
import jax
import jax.numpy as jnp
from jax import lax
from jax.experimental import pallas as pl
from jax.experimental.pallas import tpu as pltpu
from jax.sharding import Mesh
from jax.sharding import PartitionSpec as P

GROUP = 8
UNIT = 16


def early_kernel(order, srcs, locs, fresh, seg, *rest, pieces):
    inputs, (state, scales, out), (buf, acc, obuf, sems, osems) = rest[:pieces], rest[pieces:-5], rest[-5:]
    tile = buf.shape[1]
    rows = obuf.shape[1] - tile
    step_id = pl.program_id(0)
    steps = pl.num_programs(0)

    @pl.when(step_id == 0)
    def _():
        loads, place = [], 0
        for n, piece in enumerate(inputs):
            loads.append(
                pltpu.make_async_copy(piece, buf.at[pl.ds(place, piece.shape[0])], sems.at[n])
            )
            place += piece.shape[0]
        for load in loads:
            load.start()
        acc[...] = jnp.zeros_like(acc)
        for load in loads:
            load.wait()

    side = lax.rem(step_id, 2)

    def put(n, s):
        return pltpu.make_async_copy(
            obuf.at[s, pl.ds(0, rows)], out.at[pl.ds(n * rows, rows)], osems.at[s]
        )

    @pl.when(step_id >= 2)
    def _():
        put(step_id - 2, side).wait()

    obuf[side] = jnp.zeros(obuf.shape[1:], obuf.dtype)

    def step(group, carry):
        total = acc[...]
        for i in range(GROUP):
            k = group * GROUP + i
            keep = jnp.where(fresh[k] > 0, 0.0, 1.0).astype(jnp.float32)
            source = pl.multiple_of(srcs[k] * tile, tile)
            product = jnp.dot(
                buf[order[k]],
                state[pl.ds(source, tile), :],
                preferred_element_type=jnp.float32,
            )
            total = product * scales[pl.ds(k, 1), :] + total * keep
            row = pl.multiple_of(locs[k] * tile, tile)
            obuf[side, pl.ds(row, tile), :] = total.astype(obuf.dtype)
        acc[...] = total
        return carry

    lax.fori_loop(seg[step_id], seg[step_id + 1], step, 0)
    put(step_id, side).start()

    @pl.when(step_id == steps - 1)
    def _():
        put(step_id - 1, 1 - side).wait()
        put(step_id, side).wait()


def early_messages(lists, pieces, state, scales):
    order, srcs, locs, fresh, seg = lists
    tile = pieces[0].shape[1]
    width = state.shape[1]
    rows = UNIT * tile
    steps = seg.shape[0] - 1
    total = sum(piece.shape[0] for piece in pieces)
    return pl.pallas_call(
        lambda *refs: early_kernel(*refs, pieces=len(pieces)),
        grid_spec=pltpu.PrefetchScalarGridSpec(
            num_scalar_prefetch=5,
            grid=(steps,),
            in_specs=[pl.BlockSpec(memory_space=pl.ANY)] * len(pieces)
            + [
                pl.BlockSpec(state.shape, lambda i, *_: (0, 0)),
                pl.BlockSpec(scales.shape, lambda i, *_: (0, 0)),
            ],
            out_specs=pl.BlockSpec(memory_space=pl.ANY),
            scratch_shapes=[
                pltpu.VMEM((total, tile, tile), jnp.bfloat16),
                pltpu.VMEM((tile, width), jnp.float32),
                pltpu.VMEM((2, rows + tile, width), jnp.bfloat16),
                pltpu.SemaphoreType.DMA((len(pieces),)),
                pltpu.SemaphoreType.DMA((2,)),
            ],
        ),
        out_shape=jax.ShapeDtypeStruct((steps * rows, width), jnp.bfloat16),
        name="early_messages",
    )(order, srcs, locs, fresh, seg, *pieces, state, scales)


def late_kernel(order, srcs, place, fresh, last, count, *rest, pieces):
    inputs, (_, state, scales, out), (buf, ibuf, obuf, sems, isems, osems) = (
        rest[:pieces],
        rest[pieces:-6],
        rest[-6:],
    )
    tile = buf.shape[1]
    groups = count[0]

    def get(k, side, i):
        return pltpu.make_async_copy(out.at[pl.ds(place[k] * tile, tile)], ibuf.at[side, i], isems.at[side, i])

    def put(k, side, i):
        return pltpu.make_async_copy(obuf.at[side, i], out.at[pl.ds(place[k] * tile, tile)], osems.at[side, i])

    def begin(group):
        for i in range(GROUP):
            k = group * GROUP + i

            @pl.when(fresh[k] > 0)
            def _(k=k, i=i):
                get(k, lax.rem(group, 2), i).start()

    def finish(group):
        for i in range(GROUP):
            k = group * GROUP + i

            @pl.when(last[k] > 0)
            def _(k=k, i=i):
                put(k, lax.rem(group, 2), i).wait()

    @pl.when(groups > 0)
    def _():
        loads, at = [], 0
        for n, piece in enumerate(inputs):
            loads.append(pltpu.make_async_copy(piece, buf.at[pl.ds(at, piece.shape[0])], sems.at[n]))
            at += piece.shape[0]
        for load in loads:
            load.start()
        begin(0)
        for load in loads:
            load.wait()

        def step(group, total):
            side = lax.rem(group, 2)

            @pl.when(group + 1 < groups)
            def _():
                begin(group + 1)

            @pl.when(group >= 2)
            def _():
                finish(group - 2)

            for i in range(GROUP):
                k = group * GROUP + i

                @pl.when(fresh[k] > 0)
                def _(k=k, i=i):
                    get(k, side, i).wait()

            for i in range(GROUP):
                k = group * GROUP + i
                source = pl.multiple_of(srcs[k] * tile, tile)
                product = jnp.dot(
                    buf[order[k]],
                    state[pl.ds(source, tile), :],
                    preferred_element_type=jnp.float32,
                )
                before = jnp.where(fresh[k] > 0, ibuf[side, i].astype(jnp.float32), total)
                total = product * scales[pl.ds(k, 1), :] + before
                obuf[side, i] = total.astype(obuf.dtype)

            for i in range(GROUP):
                k = group * GROUP + i

                @pl.when(last[k] > 0)
                def _(k=k, i=i):
                    put(k, side, i).start()

            return total

        lax.fori_loop(0, groups, step, jnp.zeros((tile, scales.shape[1]), jnp.float32))

        @pl.when(groups >= 2)
        def _():
            finish(groups - 2)

        finish(groups - 1)


def late_messages(lists, pieces, partial, state, scales):
    tile = pieces[0].shape[1]
    width = state.shape[1]
    total = sum(piece.shape[0] for piece in pieces)
    hbm = pl.BlockSpec(memory_space=pl.ANY)
    return pl.pallas_call(
        lambda *refs: late_kernel(*refs, pieces=len(pieces)),
        grid_spec=pltpu.PrefetchScalarGridSpec(
            num_scalar_prefetch=len(lists),
            grid=(1,),
            in_specs=[hbm] * (len(pieces) + 1)
            + [
                pl.BlockSpec(state.shape, lambda i, *_: (0, 0)),
                pl.BlockSpec(scales.shape, lambda i, *_: (0, 0)),
            ],
            out_specs=hbm,
            scratch_shapes=[
                pltpu.VMEM((total, tile, tile), jnp.bfloat16),
                pltpu.VMEM((2, GROUP, tile, width), jnp.bfloat16),
                pltpu.VMEM((2, GROUP, tile, width), jnp.bfloat16),
                pltpu.SemaphoreType.DMA((len(pieces),)),
                pltpu.SemaphoreType.DMA((2, GROUP)),
                pltpu.SemaphoreType.DMA((2, GROUP)),
            ],
        ),
        out_shape=jax.ShapeDtypeStruct(partial.shape, partial.dtype),
        input_output_aliases={len(lists) + len(pieces): 0},
        name="late_messages",
    )(*lists, *pieces, partial, state, scales)


def update_kernel(
    base, query_src, own, got, query_row, weight_high, weight_low, average, rows, out
):
    count, width = own.shape
    channels = width // query_src.shape[0]
    query = lax.broadcasted_iota(jnp.int32, (1, width), 1) // channels
    target = jnp.zeros((1, width), jnp.int32)
    for q in range(query_src.shape[0]):
        target = jnp.where(query == q, query_src[q], target)
    node = lax.broadcasted_iota(jnp.int32, (count, width), 0) + (base[0] + pl.program_id(0) * count)

    def dot(left, right):
        return jnp.dot(left, right, preferred_element_type=jnp.float32)

    def split(value):
        high = value.astype(jnp.bfloat16)
        return high, (value - high.astype(jnp.float32)).astype(jnp.bfloat16)

    aggregate = own[...].astype(jnp.float32) + got[...].astype(jnp.float32)
    aggregate = aggregate + jnp.where(node == target, query_row[...], 0.0)
    high, low = split(aggregate)
    shifted = dot(high, weight_high[...]) + dot(low, weight_high[...]) + dot(high, weight_low[...])
    shifted = shifted + rows[0:1, :]
    high, low = split(shifted * shifted)
    spread = dot(high, average[...]) + dot(low, average[...])
    out[...] = jnp.maximum(rows[1:2, :] * shifted * lax.rsqrt(spread + 1e-05) + rows[2:3, :], 0.0)


def update(base, query_src, own, got, query_row, weight_high, weight_low, average, rows):
    count, width = got.shape
    steps = 4
    smem = pl.BlockSpec(memory_space=pltpu.SMEM)
    moving = pl.BlockSpec((count // steps, width), lambda i: (i, 0))
    fixed = lambda value: pl.BlockSpec(value.shape, lambda i: (0, 0))
    return pl.pallas_call(
        update_kernel,
        grid=(steps,),
        in_specs=[smem, smem, moving, moving]
        + [fixed(value) for value in (query_row, weight_high, weight_low, average, rows)],
        out_specs=moving,
        out_shape=jax.ShapeDtypeStruct((count, width), jnp.float32),
        name="update",
    )(base, query_src, own, got, query_row, weight_high, weight_low, average, rows)


def shift(value, axis, by):
    size = lax.axis_size(axis)
    return lax.ppermute(value, axis, [(i, (i + by) % size) for i in range(size)])


def along(value, by):
    size = lax.axis_size("zl")
    return lax.ppermute(value, "zl", [(i, i + by) for i in range(size) if 0 <= i + by < size])


def swap(value):
    return lax.ppermute(value, "c", [(0, 1), (1, 0)])


def local(
    state,
    tiles,
    tile_src,
    tile_dst,
    tile_rel,
    query_src,
    query_rel,
    rel_table,
    query_table,
    linear_weight,
    linear_bias,
    norm_gain,
    norm_shift,
):
    node_rows, width = state.shape
    tile = tiles.shape[1]
    channels = rel_table.shape[1]
    queries = width // channels
    owned = node_rows // tile
    outer, ny, nx = lax.axis_size("zh"), lax.axis_size("y"), lax.axis_size("x")
    owners = outer * ny * nx
    blocks = owned * owners
    at_z, at_y, at_x = lax.axis_index("zh"), lax.axis_index("y"), lax.axis_index("x")

    line, core = lax.axis_index("zl"), lax.axis_index("c")
    tcap = tiles.shape[0]
    right1, left1 = along(tiles, 1), along(tiles, -1)
    lists = lax.all_gather(jnp.stack([tile_src, tile_dst, tile_rel]), ("zl", "c"), axis=1, tiled=True)
    right1, left1, lists = lax.optimization_barrier((right1, left1, lists))
    right2, left2 = along(right1, 1), along(left1, -1)
    right3, left3 = along(right2, 1), along(left2, -1)
    one = jnp.concatenate([tiles, right1, left1])
    two = jnp.where(line >= 2, right2, left2)
    early_pieces = [one, two, swap(one), swap(two)]

    src, dst, rel = lists[0], lists[1], lists[2]

    owner, inside = dst // owned, dst % owned
    go_z = (owner // (ny * nx) - at_z) % outer
    used = dst < blocks
    bins = blocks // UNIT
    place = jnp.where(used, (owner % (ny * nx) * outer + go_z) * owned + inside, blocks)
    bin_id = place // UNIT
    loc = place % UNIT

    slots = src.shape[0]
    ids = jnp.arange(slots, dtype=jnp.int32)
    away = ids // (2 * tcap) - line
    far = jnp.abs(away)
    other = (ids // tcap % 2 != core).astype(jnp.int32)
    early = far < 3
    turn = jnp.where(away == 0, 0, jnp.where(away == -1, 1, jnp.where(away == 1, 2, 3)))
    at = jnp.where(early, (other * 4 + turn) * tcap, other * tcap) + ids % tcap

    key = place * slots + ids
    below = key[None, :] < key[:, None]
    above = key[None, :] > key[:, None]
    level = place[None, :] == place[:, None]

    def ranks(member):
        mine = jnp.logical_and(member[None, :], member[:, None])
        less = jnp.logical_and(below, mine)
        more = jnp.logical_and(above, mine)
        rank = jnp.sum(less.astype(jnp.int32), axis=1)
        first = jnp.logical_not(jnp.any(jnp.logical_and(less, level), axis=1)).astype(jnp.int32)
        last = jnp.logical_not(jnp.any(jnp.logical_and(more, level), axis=1)).astype(jnp.int32)
        return rank, first, last

    query_row = query_table[query_rel].reshape(1, width)
    state_bf = state.astype(jnp.bfloat16)

    def arrange(goal, size):
        chosen = goal[None, :] == jnp.arange(size, dtype=jnp.int32)[:, None]

        def put(values, fill):
            return jnp.sum(jnp.where(chosen, (values - fill)[None, :], 0), axis=1) + fill

        filled = jnp.any(chosen, axis=1)
        rows = jnp.where(filled[:, None], rel_table[put(rel, 0)], 0.0)
        return put, jnp.tile(rows, (1, queries)) * query_row

    member = jnp.logical_and(used, early)
    rank, first, _ = ranks(member)
    edges = jnp.arange(bins + 1, dtype=jnp.int32)
    ahead = jnp.sum(
        jnp.logical_and(member[None, :], place[None, :] < (edges * UNIT)[:, None]).astype(jnp.int32), axis=1
    )
    groups = (ahead[1:] - ahead[:-1] + GROUP - 1) // GROUP
    seg = jnp.sum(jnp.where(edges[None, :-1] < edges[:, None], groups[None, :], 0), axis=1)
    moved = seg[:-1] * GROUP - ahead[:-1]
    move = jnp.sum(
        jnp.where(jnp.minimum(bin_id, bins - 1)[:, None] == edges[None, :-1], moved[None, :], 0), axis=1
    )
    padded = slots + bins * GROUP
    put, scales = arrange(jnp.where(member, rank + move, padded), padded)
    work = (put(at, 0), put(src, 0), put(loc, UNIT), put(first, 0), seg)
    member = jnp.logical_and(used, jnp.logical_not(early))
    rank, first, last = ranks(member)
    count = jnp.sum(member.astype(jnp.int32)).reshape(1)
    padded = -(-2 * tcap // GROUP) * GROUP
    put, late_scales = arrange(jnp.where(member, rank, padded), padded)
    late = (put(at, 0), put(src, 0), put(place, 0), put(first, 0), put(last, 0), (count + GROUP - 1) // GROUP)

    late, late_scales, state_bf = lax.optimization_barrier((late, late_scales, state_bf))
    partial = early_messages(work, early_pieces, state_bf, scales)
    after, partial = lax.optimization_barrier((line, partial))
    three = jnp.where(after >= 2, right3, left3)
    partial = late_messages(late, [three, swap(three)], partial, state_bf, late_scales)
    summed = lax.psum_scatter(partial, ("y", "x"), scatter_dimension=0, tiled=True)
    got = shift(summed[node_rows:], "zh", 1)

    eye = jnp.eye(queries, dtype=jnp.float32)
    weight = jnp.kron(eye, linear_weight - jnp.mean(linear_weight, axis=1, keepdims=True))
    weight_high = weight.astype(jnp.bfloat16)
    weight_low = (weight - weight_high.astype(jnp.float32)).astype(jnp.bfloat16)
    average = jnp.kron(eye, jnp.full((channels, channels), 1.0 / channels, jnp.float32)).astype(jnp.bfloat16)
    bias = linear_bias - jnp.mean(linear_bias)
    rows = jnp.stack([jnp.tile(bias, queries), jnp.tile(norm_gain, queries), jnp.tile(norm_shift, queries)])
    shard = (at_z * ny + at_y) * nx + at_x
    first_node = (shard * node_rows).astype(jnp.int32).reshape(1)
    return update(
        first_node, query_src, summed, got, query_row, weight_high, weight_low, average, rows
    )


def solution(mesh):
    fine = Mesh(mesh.devices.reshape(2, 4, 4, 4, 2), ("zh", "y", "x", "zl", "c"))
    node = ("zh", "y", "x")
    query = ("zl", "c")
    placed = (
        P(node, query),
        P(node + query, None, None),
        P(node + query),
        P(node + query),
        P(node + query),
        P(query),
        P(query),
        P(),
        P(),
        P(),
        P(),
        P(),
        P(),
    )
    return jax.shard_map(local, mesh=fine, in_specs=placed, out_specs=P(node, query), check_vma=False)
```
